32 devices in a mesh: dom: 16 (over z, x, core), sub: 2 (over y).
Axes of the slice: x: 2, y: 2, z: 4, core: 2. Of those that a mesh axis runs over, the one named last changes fastest.
Arguments:
- density: float32 [56, 8192], P(None, ('dom', 'sub')), may hold values from -6 to 6
- mass_theta: float32 [56, 8192], P(None, ('dom', 'sub')), may hold values from -6 to 6
- momentum: float32 [56, 24576], P(None, ('dom', 'sub')), may hold values from -6 to 6
- density_forcing: float32 [56, 8192], P(None, ('dom', 'sub')), may hold values from -4 to 4
- theta_forcing: float32 [56, 8192], P(None, ('dom', 'sub')), may hold values from -4 to 4
- momentum_forcing: float32 [56, 24576], P(None, ('dom', 'sub')), may hold values from -4 to 4
- edge_theta: float32 [56, 24576], P(None, ('dom', 'sub')), may hold values from 0.5 to 1.5
- inverse_spacing: float32 [24576], P(('dom', 'sub')), may hold values from 0.5 to 2
- face_weight: float32 [6, 8192], P(None, ('dom', 'sub')), may hold values from 0.5 to 2
- edge_cells: int32 [2, 24576], P(None, ('dom', 'sub')), may hold values from 0 to 511, as said below
- cell_edges: int32 [6, 8192], P(None, ('dom', 'sub')), may hold values from 0 to 1023
- orientation: int32 [6, 8192], P(None, ('dom', 'sub')), may hold values from 0 to 1
- send_cells: int32 [32, 4, 64], P(('dom', 'sub')), may hold values from 0 to 255
- send_edges: int32 [32, 4, 64], P(('dom', 'sub')), may hold values from 0 to 767
- halo_counts: int32 [32, 4], P(('dom', 'sub')), may hold values from 1 to 64, as said below
Outputs:
- new_density: float32 [56, 8192], P(None, ('dom', 'sub'))
- new_mass_theta: float32 [56, 8192], P(None, ('dom', 'sub'))
- new_momentum: float32 [56, 24576], P(None, ('dom', 'sub'))
The draws below stay inside these ranges and needn't reach their ends.
Inputs may be any that keep to these rules, and one draw needn't show every extreme that they name: `edge_cells`: row 0 names an owned cell of the edge's partition; row 1 names an owned cell, or from 256 on ghost slot k * 64 + j of neighbour k. `cell_edges`: values below 768 are owned edges; from 768 on, ghost edge slot k * 64 + j of neighbour k. `send_cells`: local cell indices of the sending partition. `send_edges`: local edge indices of the sending partition. `halo_counts`: every count of 64 is reached by some partition in every draw; slots from the count on carry nothing.
All inputs are finite; a program needn't handle non-finite values.
Results may differ from the reference program's by a relative error of at most 0.00002.
Values sent between devices are 32-bit elements; how exact they have to be, the bound alone decides.
No kernel may reach another device: no remote copies, remote signals or barrier semaphores. Data moves between devices by JAX's collectives and lax.ppermute only.
A program may use at most 64 MiB of HBM per device.

```python
import math
import jax
import jax.numpy as jnp

LEVELS = 56
CELL_DEV = 256
HALO = 64
FACES = 6
PEERS = 4
ITERS = 4
EDGE_DEV = 768
CELLS = 8192
EDGES = 24576
DEVICES = 32


def draw_edge_cells(key, part):
    first_key = jax.random.fold_in(key, 11)
    second_key = jax.random.fold_in(key, 12)
    first = jax.random.randint(first_key, (1, DEVICES * EDGE_DEV), 0, CELL_DEV)
    second = jax.random.randint(second_key, (1, DEVICES * EDGE_DEV), 0, CELL_DEV + 4 * HALO)
    return jnp.concatenate([first, second], axis=0).astype(jnp.int32)


def draw_halo_counts(key, part):
    count_key = jax.random.fold_in(key, 21)
    place_key = jax.random.fold_in(key, 22)
    counts = jax.random.randint(count_key, (DEVICES * 4,), 1, HALO + 1)
    place = jax.random.randint(place_key, (), 0, DEVICES * 4)
    counts = jnp.where(jnp.arange(DEVICES * 4) == place, HALO, counts)
    return counts.reshape(DEVICES, 4).astype(jnp.int32)


def plant(array, own_key, least, largest):
    extent = array.shape
    index_at = [jax.random.randint(jax.random.fold_in(own_key, axis), (), 0, extent[axis]) for axis in range(len(extent))]
    array = array.at[tuple(index_at)].set(least)
    longest = extent.index(max(extent))
    index_at[longest] = (index_at[longest] + 1) % extent[longest]
    return array.at[tuple(index_at)].set(largest)


def level_of(key, extent, shards, low, largest):
    factor_of = 1.0
    for position, shards_of in shards:
        steps = jax.random.uniform(jax.random.fold_in(jax.random.fold_in(key, 6), position), (shards_of,), jnp.float32, low / len(shards), largest / len(shards))
        factor_of = factor_of * jnp.repeat(jnp.exp(steps), extent[position] // shards_of).reshape((-1,) + (1,) * (len(extent) - 1 - position))
    return factor_of


def normal_values(rng, shape, spread, limit, cuts=(), held_as=jnp.bfloat16):
    drawn = spread * jax.random.normal(rng, shape, jnp.float32)
    if cuts:
        drawn = drawn * level_of(rng, shape, cuts, -0.22, 0.18)
    return jnp.clip(drawn, -limit, limit).astype(held_as)


def setup_inputs(seed: int = 0) -> dict:
    arg_keys = jax.random.split(jax.random.key(seed), 16)
    return {
        "density": normal_values(arg_keys[0], (LEVELS, CELLS), 1.0, 6.0, ((1, 32),), jnp.float32),
        "mass_theta": normal_values(arg_keys[1], (LEVELS, CELLS), 1.0, 6.0, ((1, 32),), jnp.float32),
        "momentum": normal_values(arg_keys[2], (LEVELS, EDGES), 1.0, 6.0, ((1, 32),), jnp.float32),
        "density_forcing": normal_values(arg_keys[3], (LEVELS, CELLS), 0.5, 4.0, ((1, 32),), jnp.float32),
        "theta_forcing": normal_values(arg_keys[4], (LEVELS, CELLS), 0.5, 4.0, ((1, 32),), jnp.float32),
        "momentum_forcing": normal_values(arg_keys[5], (LEVELS, EDGES), 0.5, 4.0, ((1, 32),), jnp.float32),
        "edge_theta": jnp.clip(0.5 + 1.0 * jax.random.uniform(arg_keys[6], (LEVELS, EDGES), jnp.float32) ** level_of(arg_keys[6], (LEVELS, EDGES), ((1, 32),), -0.2, 0.2), 0.5, 1.5),
        "inverse_spacing": jnp.clip(jnp.exp(math.log(2.0) - 1.3862944 * jax.random.uniform(arg_keys[7], (EDGES,), jnp.float32) ** level_of(arg_keys[7], (EDGES,), ((0, 32),), -0.2, 0.2)), 0.5, 2.0),
        "face_weight": jnp.clip(jnp.exp(math.log(2.0) - 1.3862944 * jax.random.uniform(arg_keys[8], (FACES, CELLS), jnp.float32) ** level_of(arg_keys[8], (FACES, CELLS), ((1, 32),), -0.2, 0.2)), 0.5, 2.0),
        "edge_cells": draw_edge_cells(jax.random.fold_in(arg_keys[15], 71), 0),
        "cell_edges": plant(jax.random.randint(arg_keys[10], (FACES, CELLS), 0, EDGE_DEV + 4 * HALO), jax.random.fold_in(arg_keys[10], 1), 0, (EDGE_DEV + 4 * HALO) - 1).astype(jnp.int32),
        "orientation": plant(jax.random.randint(arg_keys[11], (FACES, CELLS), 0, 2), jax.random.fold_in(arg_keys[11], 1), 0, 1).astype(jnp.int32),
        "send_cells": plant(jax.random.randint(arg_keys[12], (DEVICES, PEERS, HALO), 0, CELL_DEV), jax.random.fold_in(arg_keys[12], 1), 0, CELL_DEV - 1).astype(jnp.int32),
        "send_edges": plant(jax.random.randint(arg_keys[13], (DEVICES, PEERS, HALO), 0, EDGE_DEV), jax.random.fold_in(arg_keys[13], 1), 0, EDGE_DEV - 1).astype(jnp.int32),
        "halo_counts": draw_halo_counts(jax.random.fold_in(arg_keys[15], 71), 0),
    }


peer_shifts = (1, -1, 2, -2)
time_step = 0.2
sound_factor = 1.0


def widen(field3, rows, counts):
    parts_count = field3.shape[1]
    width = rows.shape[2]
    here = jnp.arange(parts_count)
    pieces = [field3]
    for peer_slot in range(4):
        source = (here - peer_shifts[peer_slot]) % parts_count
        picked = rows[source, peer_slot]
        values = field3[:, source[:, None], picked]
        live_mask = (jnp.arange(width)[None, :] < counts[source, peer_slot][:, None]).astype(field3.dtype)
        pieces.append(values * live_mask[None])
    return jnp.concatenate(pieces, axis=2)


def take_one(field, index):
    return jnp.take(field, index, axis=1)


def pick(field3, index):
    return jax.vmap(take_one, in_axes=(1, 0), out_axes=1)(field3, index)


def reference(density, mass_theta, momentum, density_forcing, theta_forcing, momentum_forcing, edge_theta, inverse_spacing, face_weight, edge_cells, cell_edges, orientation, send_cells, send_edges, halo_counts):
    parts_count = DEVICES
    dens = density.reshape(LEVELS, parts_count, CELL_DEV)
    mass = mass_theta.reshape(LEVELS, parts_count, CELL_DEV)
    moment = momentum.reshape(LEVELS, parts_count, EDGE_DEV)
    dforce = density_forcing.reshape(LEVELS, parts_count, CELL_DEV)
    tforce = theta_forcing.reshape(LEVELS, parts_count, CELL_DEV)
    mforce = momentum_forcing.reshape(LEVELS, parts_count, EDGE_DEV)
    etheta = edge_theta.reshape(LEVELS, parts_count, EDGE_DEV)
    spacing = inverse_spacing.reshape(parts_count, EDGE_DEV)
    ecells = edge_cells.reshape(2, parts_count, EDGE_DEV)
    cedges = cell_edges.reshape(6, parts_count, CELL_DEV)
    signed = (face_weight * (2 * orientation - 1).astype(face_weight.dtype)).reshape(6, parts_count, CELL_DEV)
    for substep in range(ITERS):
        widened = widen(mass, send_cells, halo_counts)
        contrast = pick(widened, ecells[1]) - pick(widened, ecells[0])
        moment = moment + time_step * (mforce - sound_factor * spacing[None] * contrast)
        flux = moment * etheta
        moment_wide = widen(moment, send_edges, halo_counts)
        flux_wide = widen(flux, send_edges, halo_counts)
        mass_div = jnp.zeros_like(dens)
        theta_div = jnp.zeros_like(dens)
        for face in range(6):
            mass_div = mass_div + signed[face][None] * pick(moment_wide, cedges[face])
            theta_div = theta_div + signed[face][None] * pick(flux_wide, cedges[face])
        dens = dens + time_step * (dforce - mass_div)
        mass = mass + time_step * (tforce - theta_div)
    return (dens.reshape(LEVELS, CELLS), mass.reshape(LEVELS, CELLS), moment.reshape(LEVELS, EDGES))
```

```python
import functools

import jax
import jax.numpy as jnp
from jax import lax
from jax.experimental import pallas as pl
from jax.experimental.pallas import tpu as pltpu
from jax.sharding import PartitionSpec as P

ITERS = 4
time_step = 0.2
sound_factor = 1.0
AXES = ("dom", "sub")
F32, BF16 = jnp.float32, jnp.bfloat16


def up(n, m):
    return -(-n // m) * m


def split(x, n):
    terms = []
    for _ in range(n):
        t = x.astype(BF16)
        terms.append(t)
        x = x - t.astype(F32)
    return terms


def stack(ref, rows, parts):
    for (row, terms), blocks in parts:
        at = 0
        for b in blocks:
            for i, t in enumerate(split(b, terms)):
                ref[row + i * rows : row + i * rows + b.shape[0], at : at + b.shape[1]] = t
            at += b.shape[1]


def dot(a, b):
    return jnp.dot(a, b, preferred_element_type=F32)


def place():
    p = lax.axis_index(AXES)
    return p % 2, (p // 2) % 2


def onehot(row, n):
    w = row.shape[1]
    return lax.broadcasted_iota(jnp.int32, (n, w), 0) == row


def send_row(lists, counts, pos, odd, odd2):
    h = lists.shape[2]
    k = 2 * (pos // 2)
    flip = (odd if pos < 2 else odd2) != (pos % 2)
    j = lax.broadcasted_iota(jnp.int32, (1, h), 1)
    a = jnp.where(j < counts[0, k], lists[0, k : k + 1, :], -1)
    b = jnp.where(j < counts[0, k + 1], lists[0, k + 1 : k + 2, :], -1)
    return jnp.where(flip, b, a)


def remap(idx, own, h, odd, odd2):
    g = idx - own
    one, two = (1 - odd) * h, (1 - odd2) * h
    d = jnp.where(g < 0, 0, jnp.where(g < h, one, jnp.where(g < 2 * h, -one, jnp.where(g < 3 * h, two, -two))))
    return idx + d


def first_kernel(theta, lists, counts, *rest):
    outs, scratch = rest[:4], rest[4]
    odd, odd2 = place()
    L, C = theta.shape
    R = scratch.shape[0] // 3
    stack(scratch, R, [((0, 3), [theta[...]])])
    a = scratch[...]
    for pos in range(4):
        sel = onehot(send_row(lists, counts, pos, odd, odd2), C)
        o = dot(a, sel.astype(F32).astype(BF16))
        outs[pos][...] = o[0:L] + o[R : R + L] + o[2 * R : 2 * R + L]


def build_kernel(ec, ce, orient, weight, clists, elists, counts, d_ref, s1_ref, s2_ref, pc_ref, pe_ref):
    odd, odd2 = place()
    C = ce.shape[1]
    E = ec.shape[1]
    h = clists.shape[2]
    K = C + 4 * h
    e = remap(ec[...], C, h, odd, odd2)
    d = onehot(e[1:2], K).astype(F32) - onehot(e[0:1], K).astype(F32)
    d_ref[...] = d.astype(BF16)
    c = remap(ce[...], E, h, odd, odd2)
    signed = weight[...] * (2 * orient[...] - 1).astype(F32)
    K = E + 4 * h
    s = jnp.zeros((K, C), F32)
    for f in range(ce.shape[0]):
        s = s + jnp.where(onehot(c[f : f + 1], K), signed[f : f + 1], 0.0)
    s1 = s.astype(BF16)
    s1_ref[...] = s1
    s2_ref[...] = (s - s1.astype(F32)).astype(BF16)
    for pos in range(4):
        pc_ref[pos] = onehot(send_row(clists, counts, pos, odd, odd2), C).astype(F32).astype(BF16)
        pe_ref[pos] = onehot(send_row(elists, counts, pos, odd, odd2), E).astype(F32).astype(BF16)


def edge_kernel(with_theta, theta, g0, g1, g2, g3, m, mf, sp, et, d_ref, pe, m_out, o0, o1, o2, o3, wide, sent):
    L = theta.shape[0]
    R = wide.shape[0] // 3
    stack(wide, R, [((0, 3), [theta[...], g0[...], g1[...], g2[...], g3[...]])])
    o = dot(wide[...], d_ref[...])
    contrast = o[0:L] + o[R : R + L] + o[2 * R : 2 * R + L]
    new = m[...] + time_step * (mf[...] - sound_factor * sp[...] * contrast)
    m_out[...] = new
    parts = [((0, 3), [new])]
    if with_theta:
        parts.append(((3 * R, 3), [et[...]]))
    stack(sent, R, parts)
    for pos, out in enumerate((o0, o1, o2, o3)):
        o = dot(sent[...], pe[pos])
        out[0:L, :] = o[0:L] + o[R : R + L] + o[2 * R : 2 * R + L]
        if with_theta:
            o = o[3 * R :]
            out[L : 2 * L, :] = o[0:L] + o[R : R + L] + o[2 * R : 2 * R + L]


def cell_kernel(send, m, g0, g1, g2, g3, t0, t1, t2, t3, et, s1, s2, dens, theta, df, tf, pc, *rest):
    dens_out, theta_out = rest[:2]
    outs = rest[2:6] if send else ()
    wide = rest[-2] if send else rest[-1]
    L, C = theta.shape
    R = wide.shape[0] // 4
    ms = [m[...]] + [g[0:L, :] for g in (g0, g1, g2, g3)]
    ts = [et[...]] + [t[L : 2 * L, :] for t in (t0, t1, t2, t3)]
    fs = [a * b for a, b in zip(ms, ts)]
    at = 0
    for a, b in zip(ms, fs):
        a1, a2 = split(a, 2)
        b1, b2 = split(b, 2)
        w = a.shape[1]
        for i, v in enumerate((a1, b1, a2, b2)):
            wide[i * R : i * R + L, at : at + w] = v
        at += w
    o = dot(wide[...], s1[...])
    o2 = dot(wide[0 : 2 * R, :], s2[...])
    mdiv = o[0:L] + (o[2 * R : 2 * R + L] + o2[0:L])
    tdiv = o[R : R + L] + (o[3 * R : 3 * R + L] + o2[R : R + L])
    dens_out[...] = dens[...] + time_step * (df[...] - mdiv)
    new = theta[...] + time_step * (tf[...] - tdiv)
    theta_out[...] = new
    if send:
        sent = rest[-1]
        R = sent.shape[0] // 3
        stack(sent, R, [((0, 3), [new])])
        for pos, out in enumerate(outs):
            o = dot(sent[...], pc[pos])
            out[...] = o[0:L] + o[R : R + L] + o[2 * R : 2 * R + L]


VM = pl.BlockSpec(memory_space=pltpu.VMEM)
SM = pl.BlockSpec(memory_space=pltpu.SMEM)


def call(body, ins, outs, scratch=(), specs=None, flops=1 << 20, name=None):
    return pl.pallas_call(
        body,
        out_shape=[jax.ShapeDtypeStruct(s, d) for s, d in outs],
        in_specs=specs or [VM] * len(ins),
        out_specs=[VM] * len(outs),
        scratch_shapes=[pltpu.VMEM(s, d) for s, d in scratch],
        compiler_params=pltpu.CompilerParams(vmem_limit_bytes=16 << 20),
        cost_estimate=pl.CostEstimate(flops=flops, bytes_accessed=1 << 20, transcendentals=0),
        name=name,
    )(*ins)


def exchange(blocks, n):
    got = [None] * 4
    for pos in (1, 3, 0, 2):
        step = 1 if pos < 2 else 2
        pairs = []
        for p in range(n):
            low = (p // step) % 2 == 0
            ahead = low == (pos % 2 == 0)
            pairs.append((p, (p + step if ahead else p - step) % n))
        got[pos] = lax.ppermute(blocks[pos], AXES, pairs)
    return got


def local(n, density, mass_theta, momentum, density_forcing, theta_forcing, momentum_forcing, edge_theta,
          inverse_spacing, face_weight, edge_cells, cell_edges, orientation, send_cells, send_edges, halo_counts):
    L, C = mass_theta.shape
    E = momentum.shape[1]
    h = send_cells.shape[2]
    R = up(L, 16)
    block = ((L, h), F32)
    packed = call(first_kernel, (mass_theta, send_cells, halo_counts), [block] * 4,
                  [((3 * R, C), BF16)], [VM, VM, SM], name="first")
    ghosts = exchange(packed, n)
    d, s1, s2, pc, pe = call(
        build_kernel, (edge_cells, cell_edges, orientation, face_weight, send_cells, send_edges, halo_counts),
        [((C + 4 * h, E), BF16), ((E + 4 * h, C), BF16), ((E + 4 * h, C), BF16), ((4, C, h), BF16), ((4, E, h), BF16)],
        (), [VM] * 6 + [SM], name="build")
    sp = inverse_spacing.reshape(1, E)
    thetas = None
    for step in range(ITERS):
        first, last = step == 0, step == ITERS - 1
        k = 2 if first else 1
        momentum, *packed = call(
            functools.partial(edge_kernel, first),
            (mass_theta, *ghosts, momentum, momentum_forcing, sp, edge_theta, d, pe),
            [((L, E), F32)] + [((k * L, h), F32)] * 4,
            [((3 * R, C + 4 * h), BF16), ((3 * k * R, E), BF16)], name="edges")
        got = exchange(packed, n)
        if first:
            thetas = got
        density, mass_theta, *packed = call(
            functools.partial(cell_kernel, not last),
            (momentum, *got, *thetas, edge_theta, s1, s2, density, mass_theta, density_forcing, theta_forcing, pc),
            [((L, C), F32)] * 2 + ([] if last else [block] * 4),
            [((4 * R, E + 4 * h), BF16)] + ([] if last else [((3 * R, C), BF16)]), name="cells")
        if not last:
            ghosts = exchange(packed, n)
    return density, mass_theta, momentum


def solution(mesh):
    n = mesh.shape["dom"] * mesh.shape["sub"]
    cols = P(None, AXES)
    return jax.shard_map(
        functools.partial(local, n),
        mesh=mesh,
        in_specs=(cols,) * 7 + (P(AXES),) + (cols,) * 4 + (P(AXES, None, None),) * 2 + (P(AXES, None),),
        out_specs=(cols,) * 3,
        check_vma=False,
    )
```

```python
import functools

import jax
import jax.numpy as jnp
from jax import lax
from jax.experimental import pallas as pl
from jax.experimental.pallas import tpu as pltpu
from jax.sharding import PartitionSpec as P

ITERS = 4
SHIFTS = (1, -1, 2, -2)
time_step = 0.2
sound_factor = 1.0
AXES = ("dom", "sub")
F32, BF16, I32 = jnp.float32, jnp.bfloat16, jnp.int32

EC0, EC1, EC0S, EC1S, SP, SPS, CE, SIGN, CELLS, TABLE = 0, 3, 6, 7, 8, 11, 12, 18, 24, 32


def up(n, m):
    return -(-n // m) * m


def split(x, n):
    terms = []
    for _ in range(n):
        t = x.astype(BF16)
        terms.append(t)
        x = x - t.astype(F32)
    return terms


def dot(a, b):
    return jnp.dot(a, b, preferred_element_type=F32)


def sum3(o, rows, at=0):
    return o[at : at + rows] + o[at + rows : at + 2 * rows] + o[at + 2 * rows : at + 3 * rows]


def bits():
    p = lax.axis_index(AXES)
    return p % 2, (p // 2) % 2, (p // 4) % 2


def hot(row, n):
    w = row.shape[1]
    at = lax.broadcasted_iota(I32, (n, w), 0)
    return jnp.where(at == row.astype(I32), 1.0, 0.0)


def by_block(parts, h):
    at = lax.broadcasted_iota(I32, parts[0].shape, 1)
    out = parts[3]
    for k in (2, 1, 0):
        out = jnp.where(at < (k + 1) * h, parts[k], out)
    return out


def fetch(refs, bufs, sems):
    copies = [pltpu.make_async_copy(r, b, sems.at[i]) for i, (r, b) in enumerate(zip(refs, bufs))]
    for c in copies:
        c.start()
    return copies


def first_kernel(Q, R, *refs):
    ins, (send, keep), bufs = refs[:12], refs[12:14], refs[14:26]
    rows, stacked, light, sems = refs[26:]
    copies = fetch(ins, bufs, sems)
    theta, m, mf, et, sp, ec, ce, orient, weight, clists, elists, counts = bufs
    y, _, _ = bits()
    L, C = theta.shape
    E = m.shape[1]
    h = clists.shape[2]
    W = up(L, 16)
    for c in copies:
        c.wait()
    for k in range(4):
        live = lax.broadcasted_iota(I32, (1, h), 1) < counts[0:1, k : k + 1]
        rows[0:1, k * h : (k + 1) * h] = jnp.where(live, clists[0, k : k + 1, :], -1)
        rows[1:2, k * h : (k + 1) * h] = jnp.where(live, elists[0, k : k + 1, :], -1)
    sel = hot(rows[1:2, :], E).astype(BF16)
    for f, ref in enumerate((m, mf, et)):
        for i, t in enumerate(split(ref[...], 3)):
            stacked[(3 * f + i) * W : (3 * f + i) * W + L, :] = t
    base = 9 * W
    for j, v in enumerate((ec[0:1, :].astype(F32), ec[1:2, :].astype(F32), sp[...])):
        for i, t in enumerate(split(v, 3)):
            stacked[base + 16 * (3 * j + i) : base + 16 * (3 * j + i) + 1, :] = t
    o = dot(stacked[...], sel)
    for f in range(4):
        v = theta[...] if f == 0 else sum(o[(3 * f - 3 + i) * W : (3 * f - 3 + i) * W + L] for i in range(3))
        for q in range(4):
            light[q, f * R : f * R + Q, :] = v[q * Q : (q + 1) * Q]
            light[q, f * R + Q : (f + 1) * R, :] = jnp.zeros((R - Q, C), F32)
    for q in range(2):
        keep[q * 4 * R : (q + 1) * 4 * R, :] = light[2 * y + q]
        send[q * 4 * R : (q + 1) * 4 * R, :] = light[2 * (1 - y) + q]
    small = [sum(o[base + 16 * (3 * j + i) : base + 16 * (3 * j + i) + 1] for i in range(3)) for j in range(3)]
    signed = weight[...] * (2 * orient[...] - 1).astype(F32)
    for ref in (send, keep):
        t = ref.at[8 * R : 8 * R + TABLE]
        for b in range(E // C):
            t[EC0 + b : EC0 + b + 1, :] = ec[0:1, b * C : (b + 1) * C].astype(F32)
            t[EC1 + b : EC1 + b + 1, :] = ec[1:2, b * C : (b + 1) * C].astype(F32)
            t[SP + b : SP + b + 1, :] = sp[0:1, b * C : (b + 1) * C]
        t[EC0S : EC0S + 1, :] = small[0]
        t[EC1S : EC1S + 1, :] = small[1]
        t[SPS : SPS + 1, :] = small[2]
        t[CE : CE + 6, :] = ce[...].astype(F32)
        t[SIGN : SIGN + 6, :] = signed
        t[CELLS : CELLS + 1, :] = rows[0:1, :].astype(F32)
        t[CELLS + 1 : TABLE, :] = jnp.zeros((TABLE - CELLS - 1, C), F32)


def heavy_kernel(Q, R, *refs):
    ins, (send, keep), bufs, (whole, sems) = refs[:4], refs[4:6], refs[6:10], refs[10:]
    for c in fetch(ins, bufs, sems):
        c.wait()
    _, c, _ = bits()
    at = 0
    for b in bufs:
        w = b.shape[1]
        for q in range(4):
            whole[q, 0:Q, at : at + w] = b[q * Q : (q + 1) * Q, :]
            whole[q, Q:R, at : at + w] = jnp.zeros((R - Q, w), F32)
        at += w
    for half in range(2):
        keep[half] = whole[2 * half + c]
        send[half] = whole[2 * half + 1 - c]


def heavy_turn_kernel(kept, got, send, keep):
    y, c, _ = bits()
    for cc in range(2):
        for half in range(2):
            v = jnp.where(c == cc, kept[half], got[half])

            @pl.when(y == half)
            def _():
                keep[cc] = v

            @pl.when(y != half)
            def _():
                send[cc] = v


def light_turn_kernel(R, kept, got, send, keep):
    y, c, _ = bits()
    n = 4 * R
    for yy in range(2):
        a, b, t = (jnp.where(y == yy, kept[s, :], got[s, :]) for s in (slice(0, n), slice(n, 2 * n), slice(2 * n, 2 * n + TABLE)))
        keep[yy, 0:n, :] = jnp.where(c == 0, a, b)
        send[yy, 0:n, :] = jnp.where(c == 0, b, a)
        keep[yy, n : n + TABLE, :] = t
        send[yy, n : n + TABLE, :] = t


def edge_content_kernel(R, kept, got, to_f, to_g, theta, fields, tables):
    _, c, odd = bits()
    n = 4 * R
    for r in range(4):
        v = jnp.where(c == r // 2, kept[r % 2], got[r % 2])
        theta[r] = v[0:R]
        fields[r] = v[R:n]
        tables[r] = v[n:]
    for right in range(2):
        def put(out):
            for r in range(4):
                out[r * R : (r + 1) * R, :] = theta[r]
            at = n
            for r in (2 * right, 2 * right + 1):
                out[at : at + 3 * R, :] = fields[r]
                at += 3 * R
            for r in (2 * right, 2 * right + 1):
                for row in (EC0S, EC1S, SPS):
                    out[at : at + 1, :] = tables[r, row : row + 1, :]
                    at += 1
            for r in range(4):
                out[at : at + 1, :] = tables[r, CELLS : CELLS + 1, :]
                at += 1
            out[at:, :] = jnp.zeros((out.shape[0] - at, out.shape[1]), F32)

        @pl.when(odd == 1 - right)
        def _():
            put(to_f)

        @pl.when(odd == right)
        def _():
            put(to_g)


def build_kernel(tables, do, dg, s1, s2, pc):
    C = tables.shape[2]
    K, E = do.shape[1:]
    M = s1.shape[1]
    for r in range(4):
        for b in range(E // C):
            d = hot(tables[r, EC1 + b : EC1 + b + 1, :], K) - hot(tables[r, EC0 + b : EC0 + b + 1, :], K)
            do[r, :, b * C : (b + 1) * C] = d.astype(BF16)
        d = hot(tables[r, EC1S : EC1S + 1, :], K) - hot(tables[r, EC0S : EC0S + 1, :], K)
        dg[r] = d.astype(BF16)
        s = jnp.zeros((M, C), F32)
        at = lax.broadcasted_iota(I32, (M, C), 0)
        for f in range(6):
            s = s + jnp.where(at == tables[r, CE + f : CE + f + 1, :].astype(I32), tables[r, SIGN + f : SIGN + f + 1, :], 0.0)
        t = s.astype(BF16)
        s1[r] = t
        s2[r] = (s - t.astype(F32)).astype(BF16)
        pc[r] = hot(tables[r, CELLS : CELLS + 1, :], C).astype(BF16)


def arrive_kernel(R, f, g, kept, got, mo, mfo, eto, tf, fields, sps, dg, pc):
    y, _, odd = bits()
    C = f.shape[1]
    K = dg.shape[1]
    E = mo.shape[2]
    n = 4 * R
    for r in range(4):
        v = jnp.where(y == r % 2, kept[r // 2], got[r // 2])
        mo[r] = v[:, 0:E]
        mfo[r] = v[:, E : 2 * E]
        eto[r] = v[:, 2 * E : 3 * E]
        tf[r] = v[:, 3 * E : 3 * E + C]
    for side in range(2):
        flip = odd == 1 - side
        for j in range(2):
            at = n + 3 * R * j
            fields[2 * side + j] = jnp.where(flip, f[at : at + 3 * R, :], g[at : at + 3 * R, :])
        at = n + 6 * R
        t = jnp.where(flip, f[at : at + 16, :], g[at : at + 16, :])
        for j in range(2):
            d = hot(t[3 * j + 1 : 3 * j + 2], K) - hot(t[3 * j : 3 * j + 1], K)
            dg[2 * side + j] = d.astype(BF16)
            sps[2 * side + j : 2 * side + j + 1, :] = t[3 * j + 2 : 3 * j + 3]
        for r in range(4):
            pc[4 * side + r] = hot(t[6 + r : 7 + r], C).astype(BF16)


def step_kernel(h, last, theta, f, g, tf, acc, mo, mg, mfo, gown, gnb, eto, tables, sps, do, dg, dgn, s1, s2, pc, pcn, *rest):
    if last:
        send, keep, src, wide, both, res = rest
    else:
        theta_out, acc_out, mo_out, mg_out, src, wide, both = rest
    y, _, odd = bits()
    R, C = theta.shape[1:]
    E = mo.shape[2]
    packed = []
    for w in range(12):
        if 4 <= w < 8:
            x, sel = theta[w - 4], pc[w - 4]
        else:
            r = w % 4
            rows = slice(r * R, (r + 1) * R)
            x = jnp.where(odd == (1 if w < 4 else 0), f[rows, :], g[rows, :])
            sel = pcn[w if w < 4 else w - 4]
        for i, t in enumerate(split(x, 3)):
            src[w, i * R : (i + 1) * R, :] = t
        packed.append(dot(src[w], sel))
    ghost_m, ghost_f, own = {}, {}, {}
    for q in range(2, 10):
        wide[q - 2, :, 0:C] = src[q]
        wide[q - 2, :, C : 2 * C] = by_block([packed[q - s] for s in SHIFTS], h).astype(BF16)
        a = wide[q - 2]
        mine = 4 <= q < 8
        fields = gown.at[q - 4] if mine else gnb.at[q - 2 if q < 4 else q - 6]
        select = dg[q - 4] if mine else dgn[q - 2 if q < 4 else q - 6]
        sp = tables[q - 4, SPS : SPS + 1, :] if mine else sps[(q - 2 if q < 4 else q - 6) : (q - 1 if q < 4 else q - 5), :]
        contrast = sum3(dot(a, select), R)
        new = mg[q - 2] + time_step * (fields[R : 2 * R, :] - sound_factor * sp * contrast)
        if not last:
            mg_out[q - 2] = new
        ghost_m[q] = new
        ghost_f[q] = new * fields[2 * R : 3 * R, :]
        if mine:
            contrast = sum3(dot(a, do[q - 4]), R)
            own[q] = []
            for b in range(E // C):
                cols = slice(b * C, (b + 1) * C)
                new = mo[q - 4, :, cols] + time_step * (
                    mfo[q - 4, :, cols] - sound_factor * tables[q - 4, SP + b : SP + b + 1, :] * contrast[:, cols])
                own[q].append(new)
                if last:
                    res[q - 4, :, 2 * C + b * C : 2 * C + (b + 1) * C] = new
                else:
                    mo_out[q - 4, :, cols] = new
    for r in range(4):
        q = r + 4
        ms = own[q] + [by_block([ghost_m[q - s] for s in SHIFTS], h)]
        fs = [v * eto[r, :, b * C : (b + 1) * C] for b, v in enumerate(own[q])] + [by_block([ghost_f[q - s] for s in SHIFTS], h)]
        for b, (v, u) in enumerate(zip(ms, fs)):
            v1, v2 = split(v, 2)
            u1, u2 = split(u, 2)
            for i, t in enumerate((v1, u1, v2, u2)):
                both[r, i * R : (i + 1) * R, b * C : (b + 1) * C] = t
        o = dot(both[r], s1[r])
        o2 = dot(both[r, 0 : 2 * R, :], s2[r])
        mdiv = o[0:R] + (o[2 * R : 3 * R] + o2[0:R])
        tdiv = o[R : 2 * R] + (o[3 * R : 4 * R] + o2[R : 2 * R])
        new = theta[r] + time_step * (tf[r] - tdiv)
        if last:
            res[r, :, 0:C] = new
            res[r, :, C : 2 * C] = acc[r] + mdiv
        else:
            theta_out[r * R : (r + 1) * R, :] = new
            acc_out[r] = acc[r] + mdiv
    if last:
        for cc in range(2):
            keep[cc] = res[2 * cc + y]
            send[cc] = res[2 * cc + 1 - y]


def out_turn_kernel(kept, got, send, keep):
    y, c, _ = bits()
    for half in range(2):
        for cc in range(2):
            v = jnp.where(y == half, kept[cc], got[cc])

            @pl.when(c == cc)
            def _():
                keep[half] = v

            @pl.when(c != cc)
            def _():
                send[half] = v


def final_kernel(Q, kept, got, dens, df, dens_out, theta_out, m_out):
    _, c, _ = bits()
    C = dens.shape[1]
    for q in range(4):
        half, cc = q // 2, q % 2
        v = jnp.where(c == cc, kept[half], got[half])
        rows = slice(q * Q, (q + 1) * Q)
        theta_out[rows, :] = v[0:Q, 0:C]
        dens_out[rows, :] = dens[rows, :] + time_step * (ITERS * df[rows, :] - v[0:Q, C : 2 * C])
        m_out[rows, :] = v[0:Q, 2 * C :]


VM = pl.BlockSpec(memory_space=pltpu.VMEM)
ANY = pl.BlockSpec(memory_space=pl.ANY)


def call(body, ins, outs, scratch=(), spec=VM, name=None):
    return pl.pallas_call(
        body,
        out_shape=[jax.ShapeDtypeStruct(s, d) for s, d in outs],
        in_specs=[spec] * len(ins),
        out_specs=[VM] * len(outs),
        scratch_shapes=[s if not isinstance(s, tuple) else pltpu.VMEM(*s) for s in scratch],
        compiler_params=pltpu.CompilerParams(vmem_limit_bytes=16 << 20),
        cost_estimate=pl.CostEstimate(flops=1 << 20, bytes_accessed=1 << 20, transcendentals=0),
        name=name,
    )(*ins)


def local(n, density, mass_theta, momentum, density_forcing, theta_forcing, momentum_forcing, edge_theta,
          inverse_spacing, face_weight, edge_cells, cell_edges, orientation, send_cells, send_edges, halo_counts):
    L, C = mass_theta.shape
    E = momentum.shape[1]
    h = send_cells.shape[2]
    assert L % 4 == 0 and n % 8 == 0 and C == 4 * h and E == 3 * C
    Q = L // 4
    R = up(Q, 16)
    W = up(L, 16)
    pair = lambda step: [(p, p ^ step) for p in range(n)]
    far = [(p, (p + 4 if (p // 4) % 2 else p - 4) % n) for p in range(n)]
    swap_y = lambda x: lax.ppermute(x, AXES, pair(1))
    swap_c = lambda x: lax.ppermute(x, AXES, pair(2))
    swap_f = lambda x: lax.ppermute(x, AXES, pair(4))
    swap_g = lambda x: lax.ppermute(x, AXES, far)
    ins = (mass_theta, momentum, momentum_forcing, edge_theta, inverse_spacing.reshape(1, E), edge_cells, cell_edges,
           orientation, face_weight, send_cells, send_edges, halo_counts)
    send, keep = call(
        functools.partial(first_kernel, Q, R), ins, [((8 * R + TABLE, C), F32)] * 2,
        [(a.shape, a.dtype) for a in ins] + [((8, C), I32), ((9 * W + 144, E), BF16), ((4, 4 * R, C), F32),
                                             pltpu.SemaphoreType.DMA((len(ins),))], ANY, "first")
    got = swap_y(send)
    ins = (momentum, momentum_forcing, edge_theta, theta_forcing)
    H = 3 * E + C
    hsend, hkeep = call(
        functools.partial(heavy_kernel, Q, R), ins, [((2, R, H), F32)] * 2,
        [(a.shape, a.dtype) for a in ins] + [((4, R, H), F32), pltpu.SemaphoreType.DMA((4,))], ANY, "heavy")
    hgot = swap_c(hsend)
    hsend, hkeep = call(heavy_turn_kernel, (hkeep, hgot), [((2, R, H), F32)] * 2, name="heavy_turn")
    hgot = swap_y(hsend)
    send, keep = call(functools.partial(light_turn_kernel, R), (keep, got), [((2, 4 * R + TABLE, C), F32)] * 2, name="light_turn")
    got = swap_c(send)
    to_f, to_g, theta, gown, tables = call(
        functools.partial(edge_content_kernel, R), (keep, got),
        [((10 * R + 16, C), F32)] * 2 + [((4, R, C), F32), ((4, 3 * R, C), F32), ((4, TABLE, C), F32)], name="content")
    f, g = swap_f(to_f), swap_g(to_g)
    K, M = 2 * C, E + C
    do, dg, s1, s2, pc = call(
        build_kernel, (tables,),
        [((4, K, E), BF16), ((4, K, C), BF16), ((4, M, C), BF16), ((4, M, C), BF16), ((4, C, C), BF16)], name="build")
    mo, mfo, eto, tf, gnb, sps, dgn, pcn = call(
        functools.partial(arrive_kernel, R), (f, g, hkeep, hgot),
        [((4, R, E), F32)] * 3 + [((4, R, C), F32), ((4, 3 * R, C), F32), ((8, C), F32), ((4, K, C), BF16), ((8, C, C), BF16)],
        name="arrive")
    mg = jnp.concatenate([gnb[0:2, 0:R], gown[:, 0:R], gnb[2:4, 0:R]], 0)
    acc = jnp.zeros((4, R, C), F32)
    for step in range(ITERS):
        last = step == ITERS - 1
        outs = ([((2, R, 2 * C + E), F32)] * 2 if last else
                [((4 * R, C), F32), ((4, R, C), F32), ((4, R, E), F32), ((8, R, C), F32)])
        outs = call(
            functools.partial(step_kernel, h, last),
            (theta, f, g, tf, acc, mo, mg, mfo, gown, gnb, eto, tables, sps, do, dg, dgn, s1, s2, pc, pcn), outs,
            [((12, 3 * R, C), BF16), ((8, 3 * R, K), BF16), ((4, 4 * R, M), BF16)] + ([((4, R, 2 * C + E), F32)] if last else []),
            name="step")
        if not last:
            flat, acc, mo, mg = outs
            f, g = swap_f(flat), swap_g(flat)
            theta = flat.reshape(4, R, C)
    send, keep = outs
    got = swap_y(send)
    send, keep = call(out_turn_kernel, (keep, got), [((2, R, 2 * C + E), F32)] * 2, name="out_turn")
    got = swap_c(send)
    return tuple(call(functools.partial(final_kernel, Q), (keep, got, density, density_forcing),
                      [((L, C), F32), ((L, C), F32), ((L, E), F32)], name="final"))


def solution(mesh):
    n = mesh.shape["dom"] * mesh.shape["sub"]
    cols = P(None, AXES)
    return jax.shard_map(
        functools.partial(local, n),
        mesh=mesh,
        in_specs=(cols,) * 7 + (P(AXES),) + (cols,) * 4 + (P(AXES, None, None),) * 2 + (P(AXES, None),),
        out_specs=(cols,) * 3,
        check_vma=False,
    )
```
